32 devices in a mesh: row: 4 (over y, x), col: 8 (over z, core).
Axes of the slice: x: 2, y: 2, z: 4, core: 2. Of those that a mesh axis runs over, the one named last changes fastest.
Arguments:
- features: bfloat16 [16384, 256], P(('col', 'row')), may hold values from -6 to 6
- weight: bfloat16 [256, 256], replicated, may hold values from -0.375 to 0.375
- cotangent: bfloat16 [16384, 256], P(('row', 'col')), may hold values from -6 to 6
- block_index: int32 [4, 8, 32], P('row', 'col'), may hold values from 0 to 511, as said below
- block_count: int32 [4, 8], P('row', 'col'), may hold values from 1 to 32, as said below
- block_values: bfloat16 [4, 8, 32, 128, 128], P('row', 'col'), may hold values from -0.25 to 0.25
Outputs:
- hidden_out: bfloat16 [16384, 256], P(('row', 'col'))
- input_grad: bfloat16 [16384, 256], P(('col', 'row'))
- weight_grad: float32 [256, 256], replicated
The draws below stay inside these ranges and needn't reach their ends.
Inputs may be any that keep to these rules, and one draw needn't show every extreme that they name: `block_index`: the 32 entries of one tile are distinct; slots at or after the tile's count hold blocks that are not used. `block_count`: at least one tile holds exactly 32 blocks.
All inputs are finite; a program needn't handle non-finite values.
Results may differ from the reference program's by a relative error of at most 0.015.
Values may be sent and summed in bfloat16 or wider, within the bound.
No kernel may reach another device: no remote copies, remote signals or barrier semaphores. Data moves between devices by JAX's collectives and lax.ppermute only.
A program may use at most 64 MiB of HBM per device.

```python
import math
import jax
import jax.numpy as jnp
from jax import lax

D = 256
BS = 128
GROUP = 32
BR = 32
MAXB = 32
BC = 16
NODES = 16384
FANIN = 512
N_ROW = 4
N_COL = 8


def draw_block_index(key, part):
    keys = jax.random.split(jax.random.fold_in(key, 11), N_ROW * N_COL)

    def one_tile(tile_key):
        return jax.random.permutation(tile_key, BR * BC)[:MAXB].astype(jnp.int32)
    return jax.vmap(one_tile)(keys).reshape(N_ROW, N_COL, MAXB)


def draw_block_count(key, part):
    base = jax.random.fold_in(key, 23)
    first_key, second_key, third_key = jax.random.split(base, 3)
    first = jax.random.randint(first_key, (N_ROW * N_COL,), 0, 17)
    second = jax.random.randint(second_key, (N_ROW * N_COL,), 0, 17)
    counts = MAXB // 4 + (MAXB - MAXB // 4) * first * second // 256
    counts = jnp.maximum(counts, 1)
    chosen = jax.random.randint(third_key, (), 0, N_ROW * N_COL)
    counts = counts.at[chosen].set(MAXB)
    return counts.astype(jnp.int32).reshape(N_ROW, N_COL)


def steps_of(key, extent, shards, low, top_value):
    def one(axis_at, shards_of):
        steps = jax.random.uniform(jax.random.fold_in(jax.random.fold_in(key, 6), axis_at), (shards_of,), jnp.float32, low / len(shards), top_value / len(shards))
        return jnp.repeat(jnp.exp(steps), extent[axis_at] // shards_of).reshape((-1,) + (1,) * (len(extent) - axis_at - 1))

    level = one(*shards[0])
    for cut in shards[1:]:
        level = level * one(*cut)
    return level


def noise(stream_key, shape, scale, most, cuts=(), held_as=jnp.bfloat16):
    result = scale * jax.random.normal(stream_key, shape, jnp.float32)
    if cuts:
        result = result * steps_of(stream_key, shape, cuts, -0.22, 0.18)
    return jnp.clip(result, -most, most).astype(held_as)


def setup_inputs(seed: int = 0) -> dict:
    key_list = jax.random.split(jax.random.key(seed), 7)
    return {
        "features": noise(key_list[0], (NODES, D), 1.0, 6.0, ((0, 32),)),
        "weight": noise(key_list[1], (D, D), D ** -0.5, 0.375),
        "cotangent": noise(key_list[2], (NODES, D), 1.0, 6.0, ((0, 32),)),
        "block_index": draw_block_index(jax.random.fold_in(key_list[6], 71), 0),
        "block_count": draw_block_count(jax.random.fold_in(key_list[6], 71), 0),
        "block_values": noise(key_list[5], (N_ROW, N_COL, MAXB, BS, BS), FANIN ** -0.5, 0.25, ((0, 4), (1, 8))),
    }


def forward_tile(blocks_in, values, index, count, rows_out):
    ncols = blocks_in.shape[0]
    size = blocks_in.shape[1]
    width = blocks_in.shape[2]
    lanes = jnp.arange(GROUP, dtype=jnp.int32)
    targets = jnp.arange(rows_out, dtype=jnp.int32)

    def advance(group_id, totals):
        start = (group_id * GROUP).astype(jnp.int32)
        group_values = lax.dynamic_slice_in_dim(values, start, GROUP, 0)
        group_ids = lax.dynamic_slice_in_dim(index, start, GROUP, 0).astype(jnp.int32)
        live = start + lanes < count
        picked = jnp.take(blocks_in, group_ids % ncols, axis=0)
        product = jnp.einsum('gij,gjd->gid', group_values.astype(jnp.float32), picked.astype(jnp.float32), precision=lax.Precision.HIGHEST)
        selector = ((group_ids // ncols)[None, :] == targets[:, None]) & live[None, :]
        return totals + jnp.einsum('rg,gid->rid', selector.astype(jnp.float32), product, precision=lax.Precision.HIGHEST)
    zeros = jnp.zeros((rows_out, size, width), jnp.float32)
    groups = ((count + GROUP - 1) // GROUP).astype(jnp.int32)
    return lax.fori_loop(jnp.int32(0), groups, advance, zeros)

def backward_tile(blocks_grad, values, index, count, cols_out):
    size = blocks_grad.shape[1]
    width = blocks_grad.shape[2]
    lanes = jnp.arange(GROUP, dtype=jnp.int32)
    targets = jnp.arange(cols_out, dtype=jnp.int32)

    def advance(group_id, totals):
        start = (group_id * GROUP).astype(jnp.int32)
        group_values = lax.dynamic_slice_in_dim(values, start, GROUP, 0)
        group_ids = lax.dynamic_slice_in_dim(index, start, GROUP, 0).astype(jnp.int32)
        live = start + lanes < count
        picked = jnp.take(blocks_grad, group_ids // cols_out, axis=0)
        product = jnp.einsum('gij,gid->gjd', group_values.astype(jnp.float32), picked.astype(jnp.float32), precision=lax.Precision.HIGHEST)
        selector = ((group_ids % cols_out)[None, :] == targets[:, None]) & live[None, :]
        return totals + jnp.einsum('cg,gjd->cjd', selector.astype(jnp.float32), product, precision=lax.Precision.HIGHEST)
    zeros = jnp.zeros((cols_out, size, width), jnp.float32)
    groups = ((count + GROUP - 1) // GROUP).astype(jnp.int32)
    return lax.fori_loop(jnp.int32(0), groups, advance, zeros)

def reference(features, weight, cotangent, block_index, block_count, block_values):
    projected = jnp.dot(features, weight, preferred_element_type=jnp.float32).astype(jnp.bfloat16)
    total_blocks = BR * N_ROW
    proj_blocks = projected.reshape(total_blocks, BS, D)
    grad_blocks = cotangent.reshape(total_blocks, BS, D)
    tiles = N_ROW * N_COL
    flat_index = block_index.reshape(tiles, MAXB)
    flat_count = block_count.reshape(tiles)
    flat_values = block_values.reshape(tiles, MAXB, BS, BS)

    def visit(tile, carry):
        out_acc, back_acc = carry
        tile = tile.astype(jnp.int32)
        row_start = (tile // N_COL * BR).astype(jnp.int32)
        col_start = (tile % N_COL * BC).astype(jnp.int32)
        values = lax.dynamic_index_in_dim(flat_values, tile, 0, keepdims=False)
        index = lax.dynamic_index_in_dim(flat_index, tile, 0, keepdims=False)
        count = lax.dynamic_index_in_dim(flat_count, tile, 0, keepdims=False)
        inputs = lax.dynamic_slice_in_dim(proj_blocks, col_start, BC, 0)
        part = forward_tile(inputs, values, index, count, BR)
        rounded = lax.optimization_barrier(part.astype(jnp.bfloat16)).astype(jnp.float32)
        current = lax.dynamic_slice_in_dim(out_acc, row_start, BR, 0)
        out_acc = lax.dynamic_update_slice_in_dim(out_acc, current + rounded, row_start, 0)
        grads = lax.dynamic_slice_in_dim(grad_blocks, row_start, BR, 0)
        back = backward_tile(grads, values, index, count, BC)
        back_rounded = lax.optimization_barrier(back.astype(jnp.bfloat16)).astype(jnp.float32)
        current_back = lax.dynamic_slice_in_dim(back_acc, col_start, BC, 0)
        back_acc = lax.dynamic_update_slice_in_dim(back_acc, current_back + back_rounded, col_start, 0)
        return (out_acc, back_acc)
    zeros = jnp.zeros((total_blocks, BS, D), jnp.float32)
    out_acc, back_acc = lax.fori_loop(jnp.int32(0), jnp.int32(tiles), visit, (zeros, zeros))
    hidden_out = out_acc.reshape(NODES, D).astype(jnp.bfloat16)
    grad_sum = back_acc.reshape(NODES, D)
    input_grad = jnp.dot(grad_sum, weight.astype(jnp.float32).T, precision=lax.Precision.HIGHEST).astype(jnp.bfloat16)
    weight_grad = jnp.dot(features.astype(jnp.float32).T, grad_sum, precision=lax.Precision.HIGHEST) / math.sqrt(NODES)
    return (hidden_out, input_grad, weight_grad)
```

```python
import functools
import math

import jax
import jax.numpy as jnp
from jax import lax
from jax.experimental import pallas as pl
from jax.experimental.pallas import tpu as pltpu
from jax.sharding import PartitionSpec as P


AXES = ("row", "col")
F32 = jnp.float32
BF16 = jnp.bfloat16
UNROLL = 4
ANY = pl.BlockSpec(memory_space=pl.ANY)
VMEM = pl.BlockSpec(memory_space=pltpu.VMEM)
SMEM = pl.BlockSpec(memory_space=pltpu.SMEM)


def move(x, rows, cols, fn):
    pairs = []
    for r in range(rows):
        for c in range(cols):
            to = fn(r, c)
            if to is not None:
                pairs.append((r * cols + c, to[0] * cols + to[1]))
    return lax.ppermute(x, AXES, pairs)


def fwd_kernel(nrow, ncol, idx0, idx1, cnt0, cnt1, vals0, vals1, *rest):
    shards = rest[:2 * nrow]
    zs = ncol // 2
    outs = rest[2 * nrow:2 * nrow + zs]
    vbuf, fbuf, acc, todo, sem = rest[2 * nrow + zs:]
    slots, size = vals0.shape[0], vals0.shape[1]
    rows, _ = shards[0].shape
    per = rows // size
    block_cols = nrow * per
    full = zs * rows
    me_r = lax.axis_index("row")
    me_c = lax.axis_index("col")
    me_z, me_k = me_c // 2, me_c % 2
    copies = []
    for t, vals in enumerate((vals0, vals1)):
        copies.append(pltpu.make_async_copy(vals, vbuf.at[pl.ds(t * slots, slots)], sem.at[2 * nrow + t]))
        for s in range(nrow):
            at = pl.multiple_of((me_r ^ s) * rows + t * nrow * rows, rows)
            n = t * nrow + s
            copies.append(pltpu.make_async_copy(shards[n], fbuf.at[pl.ds(at, rows)], sem.at[n]))
    for copy in copies:
        copy.start()
    acc[...] = jnp.zeros_like(acc)

    def listed(t, idx, cnt, n):
        def one(g, n):
            q = idx[g]
            br, bc = q // block_cols, q % block_cols
            owner = br // per
            todo[0, n] = t * slots + g
            todo[1, n] = t * nrow * rows + bc * size
            todo[2, n] = ((owner // 2) ^ me_z) * rows + (br % per) * size
            return n + jnp.where(owner % 2 == me_k, 1, 0)

        return lax.fori_loop(0, cnt[0], one, n)

    count = listed(1, idx1, cnt1, listed(0, idx0, cnt0, 0))
    for u in range(UNROLL):
        todo[0, count + u] = 0
        todo[1, count + u] = 0
        todo[2, count + u] = full
    for copy in copies:
        copy.wait()

    def group(i, carry):
        prods = []
        for u in range(UNROLL):
            g = i * UNROLL + u
            block = fbuf[pl.ds(pl.multiple_of(todo[1, g], size), size), :]
            prods.append((pl.multiple_of(todo[2, g], size), jnp.dot(vbuf[todo[0, g]], block, preferred_element_type=F32)))
        for at, out in prods:
            acc[pl.ds(at, size), :] += out
        return carry

    lax.fori_loop(0, (count + UNROLL - 1) // UNROLL, group, 0)
    for s in range(zs):
        outs[s][...] = acc[s * rows:(s + 1) * rows, :].astype(BF16)


def bwd_kernel(nrow, ncol, idx, cnt, vals, *rest):
    feats = rest[:nrow]
    cots = rest[nrow:nrow + ncol]
    outs = rest[nrow + ncol:2 * nrow + ncol]
    tkeep, tsend, vbuf, fbuf, cbuf, acc, tbuf, sem = rest[2 * nrow + ncol:]
    size = vals.shape[1]
    rows, width = feats[0].shape
    per = rows // size
    block_cols = nrow * per
    full = nrow * rows
    me_r = lax.axis_index("row")
    me_c = lax.axis_index("col")
    me_k = me_c % 2
    copies = [pltpu.make_async_copy(vals, vbuf, sem.at[nrow + ncol])]
    for s in range(nrow):
        copies.append(pltpu.make_async_copy(feats[s], fbuf.at[pl.ds(s * rows, rows)], sem.at[s]))
    for s in range(ncol):
        at = pl.multiple_of((me_c ^ s) * rows, rows)
        copies.append(pltpu.make_async_copy(cots[s], cbuf.at[pl.ds(at, rows)], sem.at[nrow + s]))
    for copy in copies:
        copy.start()
    acc[...] = jnp.zeros_like(acc)
    for copy in copies:
        copy.wait()
    count = cnt[0]

    def group(i, carry):
        prods = []
        for u in range(UNROLL):
            g = i * UNROLL + u
            q = idx[g]
            br, bc = q // block_cols, q % block_cols
            at = ((bc // per) ^ me_r) * rows + (bc % per) * size
            at = pl.multiple_of(jnp.where(g < count, at, full), size)
            block = cbuf[pl.ds(pl.multiple_of(br * size, size), size), :]
            prods.append((at, lax.dot_general(vbuf[g], block, (((0,), (0,)), ((), ())), preferred_element_type=F32)))
        for at, out in prods:
            acc[pl.ds(at, size), :] += out
        return carry

    lax.fori_loop(0, (count + UNROLL - 1) // UNROLL, group, 0)
    term = jnp.zeros((width, width), F32)
    for s in range(nrow):
        back = acc[s * rows:(s + 1) * rows, :].astype(BF16)
        outs[s][...] = back
        term += lax.dot_general(
            fbuf[s * rows:(s + 1) * rows, :], back, (((0,), (0,)), ((), ())), preferred_element_type=F32
        )
    tbuf[...] = term
    part = width // 2
    tkeep[...] = tbuf[pl.ds(pl.multiple_of(me_k * part, part), part), :].astype(BF16)
    tsend[...] = tbuf[pl.ds(pl.multiple_of((1 - me_k) * part, part), part), :].astype(BF16)


def split_dot(x, w, dims):
    hi = x.astype(BF16)
    lo = (x - hi.astype(F32)).astype(BF16)
    return lax.dot_general(hi, w, dims, preferred_element_type=F32) + lax.dot_general(
        lo, w, dims, preferred_element_type=F32
    )


def sum_dot_kernel(parts, dims, w, *rest):
    total = rest[0][...].astype(F32)
    for s in range(1, parts):
        total += rest[s][...].astype(F32)
    rest[parts][...] = split_dot(total, w[...], dims).astype(BF16)


def join_kernel(nodes, mine, other, out):
    part = mine.shape[0]
    me_k = lax.axis_index("col") % 2
    out[pl.ds(pl.multiple_of(me_k * part, part), part), :] = mine[...].astype(F32) / math.sqrt(nodes)
    out[pl.ds(pl.multiple_of((1 - me_k) * part, part), part), :] = other[...].astype(F32) / math.sqrt(nodes)


def bits(n):
    return [1 << b for b in range(n.bit_length() - 1)]


def body(features, weight, cotangent, block_index, block_count, block_values):
    nrow, ncol = lax.axis_size("row"), lax.axis_size("col")
    rows, width = features.shape
    size = block_values.shape[-1]
    slots = block_values.shape[2]
    zs = ncol // 2
    part = width // 2
    shape = jax.ShapeDtypeStruct

    def over_row(x, s):
        return move(x, nrow, ncol, lambda r, c: (r ^ s, c))

    def over_col(x, s):
        return move(x, nrow, ncol, lambda r, c: (r, c ^ s))

    idx = block_index.reshape(slots)
    cnt = block_count.reshape(1)
    vals = block_values.reshape(slots, size, size)
    vals1 = over_col(vals, 1)
    idx1 = over_col(idx, 1)
    cnt1 = over_col(cnt, 1)
    cots = [cotangent, over_col(cotangent, 1)]
    feats = [features] + [over_row(features, s) for s in range(1, nrow)]
    for s in range(1, zs):
        got = over_col(cotangent, 2 * s)
        cots += [got, over_col(got, 1)]
    feats1 = [over_col(feats[s], 1) for s in range(nrow)]

    parts = pl.pallas_call(
        functools.partial(fwd_kernel, nrow, ncol),
        out_shape=[shape((rows, width), BF16)] * zs,
        in_specs=[SMEM] * 4 + [ANY] * (2 + 2 * nrow),
        out_specs=[VMEM] * zs,
        scratch_shapes=[
            pltpu.VMEM((2 * slots, size, size), BF16),
            pltpu.VMEM((2 * nrow * rows, width), BF16),
            pltpu.VMEM((zs * rows + size, width), F32),
            pltpu.SMEM((3, 2 * slots + UNROLL), jnp.int32),
            pltpu.SemaphoreType.DMA((2 * nrow + 2,)),
        ],
        compiler_params=pltpu.CompilerParams(vmem_limit_bytes=16 << 20),
        name="fwd_tile",
    )(idx, idx1, cnt, cnt1, vals, vals1, *feats, *feats1)
    parts = [parts[0]] + [over_col(parts[s], 2 * s) for s in range(1, zs)]
    hidden = pl.pallas_call(
        functools.partial(sum_dot_kernel, zs, (((1,), (0,)), ((), ()))),
        out_shape=shape((rows, width), BF16),
        in_specs=[VMEM] * (1 + zs),
        out_specs=VMEM,
        compiler_params=pltpu.CompilerParams(vmem_limit_bytes=8 << 20),
        name="hidden",
    )(weight, *parts)

    out = pl.pallas_call(
        functools.partial(bwd_kernel, nrow, ncol),
        out_shape=[shape((rows, width), BF16)] * nrow + [shape((part, width), BF16)] * 2,
        in_specs=[SMEM, SMEM] + [ANY] * (1 + nrow + ncol),
        out_specs=[VMEM] * (nrow + 2),
        scratch_shapes=[
            pltpu.VMEM((slots, size, size), BF16),
            pltpu.VMEM((nrow * rows, width), BF16),
            pltpu.VMEM((ncol * rows, width), BF16),
            pltpu.VMEM((nrow * rows + size, width), F32),
            pltpu.VMEM((width, width), F32),
            pltpu.SemaphoreType.DMA((nrow + ncol + 1,)),
        ],
        compiler_params=pltpu.CompilerParams(vmem_limit_bytes=16 << 20),
        name="bwd_tile",
    )(idx, cnt, vals, *feats, *cots)
    backs, term, send = out[:nrow], out[nrow], out[nrow + 1]
    backs = [backs[0]] + [over_row(backs[s], s) for s in range(1, nrow)]
    input_grad = pl.pallas_call(
        functools.partial(sum_dot_kernel, nrow, (((1,), (1,)), ((), ()))),
        out_shape=shape((rows, width), BF16),
        in_specs=[VMEM] * (1 + nrow),
        out_specs=VMEM,
        compiler_params=pltpu.CompilerParams(vmem_limit_bytes=8 << 20),
        name="input_grad",
    )(weight, *backs)

    term = term + over_col(send, 1)
    for s in bits(nrow):
        term = term + over_row(term, s)
    for s in bits(zs):
        term = term + over_col(term, 2 * s)
    weight_grad = pl.pallas_call(
        functools.partial(join_kernel, rows * nrow * ncol),
        out_shape=shape((width, width), F32),
        in_specs=[VMEM, VMEM],
        out_specs=VMEM,
        compiler_params=pltpu.CompilerParams(vmem_limit_bytes=8 << 20),
        name="weight_grad",
    )(term, over_col(term, 1))
    return (hidden, input_grad, weight_grad)


def solution(mesh):
    in_specs = (
        P(("col", "row"), None),
        P(),
        P(("row", "col"), None),
        P("row", "col", None),
        P("row", "col"),
        P("row", "col", None, None, None),
    )
    out_specs = (P(("row", "col"), None), P(("col", "row"), None), P())

    return jax.shard_map(body, mesh=mesh, in_specs=in_specs, out_specs=out_specs, check_vma=False)
```

```python
import functools
import math

import jax
import jax.numpy as jnp
from jax import lax
from jax.experimental import pallas as pl
from jax.experimental.pallas import tpu as pltpu
from jax.sharding import PartitionSpec as P


AXES = ("row", "col")
F32 = jnp.float32
BF16 = jnp.bfloat16
UNROLL = 4
ANY = pl.BlockSpec(memory_space=pl.ANY)
HBM = pl.BlockSpec(memory_space=pltpu.HBM)
VMEM = pl.BlockSpec(memory_space=pltpu.VMEM)
SMEM = pl.BlockSpec(memory_space=pltpu.SMEM)


def move(x, rows, cols, fn):
    pairs = []
    for r in range(rows):
        for c in range(cols):
            to = fn(r, c)
            if to is not None:
                pairs.append((r * cols + c, to[0] * cols + to[1]))
    return lax.ppermute(x, AXES, pairs)


def fwd_kernel(nrow, ncol, idx0, idx1, cnt0, cnt1, vals0, vals1, *rest):
    shards = rest[:2 * nrow]
    zs = ncol // 2
    outs = rest[2 * nrow:2 * nrow + zs]
    vbuf, fbuf, acc, todo, sem = rest[2 * nrow + zs:]
    slots, size = vals0.shape[0], vals0.shape[1]
    rows, _ = shards[0].shape
    per = rows // size
    block_cols = nrow * per
    full = zs * rows
    me_r = lax.axis_index("row")
    me_c = lax.axis_index("col")
    me_z, me_k = me_c // 2, me_c % 2
    copies = []
    for t, vals in enumerate((vals0, vals1)):
        copies.append(pltpu.make_async_copy(vals, vbuf.at[pl.ds(t * slots, slots)], sem.at[2 * nrow + t]))
        for s in range(nrow):
            at = pl.multiple_of((me_r ^ s) * rows + t * nrow * rows, rows)
            n = t * nrow + s
            copies.append(pltpu.make_async_copy(shards[n], fbuf.at[pl.ds(at, rows)], sem.at[n]))
    for copy in copies:
        copy.start()
    acc[...] = jnp.zeros_like(acc)

    def listed(t, idx, cnt, n):
        def one(g, n):
            q = idx[g]
            br, bc = q // block_cols, q % block_cols
            owner = br // per
            todo[0, n] = t * slots + g
            todo[1, n] = t * nrow * rows + bc * size
            todo[2, n] = ((owner // 2) ^ me_z) * rows + (br % per) * size
            return n + jnp.where(owner % 2 == me_k, 1, 0)

        return lax.fori_loop(0, cnt[0], one, n)

    count = listed(1, idx1, cnt1, listed(0, idx0, cnt0, 0))
    for u in range(UNROLL):
        todo[0, count + u] = 0
        todo[1, count + u] = 0
        todo[2, count + u] = full
    for copy in copies:
        copy.wait()

    def group(i, carry):
        prods = []
        for u in range(UNROLL):
            g = i * UNROLL + u
            block = fbuf[pl.ds(pl.multiple_of(todo[1, g], size), size), :]
            prods.append((pl.multiple_of(todo[2, g], size), jnp.dot(vbuf[todo[0, g]], block, preferred_element_type=F32)))
        for at, out in prods:
            acc[pl.ds(at, size), :] += out
        return carry

    lax.fori_loop(0, (count + UNROLL - 1) // UNROLL, group, 0)
    for s in range(zs):
        outs[s][...] = acc[s * rows:(s + 1) * rows, :].astype(BF16)


def bwd_kernel(nrow, ncol, idx, cnt, vals, *rest):
    feats = rest[:nrow]
    cots = rest[nrow:nrow + ncol]
    outs = rest[nrow + ncol:2 * nrow + ncol]
    tkeep, tsend, vbuf, fbuf, cbuf, acc, tbuf, sem = rest[2 * nrow + ncol:]
    size = vals.shape[1]
    rows, width = feats[0].shape
    per = rows // size
    block_cols = nrow * per
    full = nrow * rows
    me_r = lax.axis_index("row")
    me_c = lax.axis_index("col")
    me_k = me_c % 2
    copies = [pltpu.make_async_copy(vals, vbuf, sem.at[nrow + ncol])]
    for s in range(nrow):
        copies.append(pltpu.make_async_copy(feats[s], fbuf.at[pl.ds(s * rows, rows)], sem.at[s]))
    for s in range(ncol):
        at = pl.multiple_of((me_c ^ s) * rows, rows)
        copies.append(pltpu.make_async_copy(cots[s], cbuf.at[pl.ds(at, rows)], sem.at[nrow + s]))
    for copy in copies:
        copy.start()
    acc[...] = jnp.zeros_like(acc)
    for copy in copies:
        copy.wait()
    count = cnt[0]

    def group(i, carry):
        prods = []
        for u in range(UNROLL):
            g = i * UNROLL + u
            q = idx[g]
            br, bc = q // block_cols, q % block_cols
            at = ((bc // per) ^ me_r) * rows + (bc % per) * size
            at = pl.multiple_of(jnp.where(g < count, at, full), size)
            block = cbuf[pl.ds(pl.multiple_of(br * size, size), size), :]
            prods.append((at, lax.dot_general(vbuf[g], block, (((0,), (0,)), ((), ())), preferred_element_type=F32)))
        for at, out in prods:
            acc[pl.ds(at, size), :] += out
        return carry

    lax.fori_loop(0, (count + UNROLL - 1) // UNROLL, group, 0)
    term = jnp.zeros((width, width), F32)
    for s in range(nrow):
        back = acc[s * rows:(s + 1) * rows, :].astype(BF16)
        outs[s][...] = back
        term += lax.dot_general(
            fbuf[s * rows:(s + 1) * rows, :], back, (((0,), (0,)), ((), ())), preferred_element_type=F32
        )
    tbuf[...] = term
    part = width // 2
    tkeep[...] = tbuf[pl.ds(pl.multiple_of(me_k * part, part), part), :].astype(BF16)
    tsend[...] = tbuf[pl.ds(pl.multiple_of((1 - me_k) * part, part), part), :].astype(BF16)


def split_dot(x, w, dims):
    hi = x.astype(BF16)
    lo = (x - hi.astype(F32)).astype(BF16)
    return lax.dot_general(hi, w, dims, preferred_element_type=F32) + lax.dot_general(
        lo, w, dims, preferred_element_type=F32
    )


def sum_dot_kernel(parts, dims, w, *rest):
    total = rest[0][...].astype(F32)
    for s in range(1, parts):
        total += rest[s][...].astype(F32)
    rest[parts][...] = split_dot(total, w[...], dims).astype(BF16)


def join_kernel(nodes, mine, other, out):
    part = mine.shape[0]
    me_k = lax.axis_index("col") % 2
    out[pl.ds(pl.multiple_of(me_k * part, part), part), :] = mine[...].astype(F32) / math.sqrt(nodes)
    out[pl.ds(pl.multiple_of((1 - me_k) * part, part), part), :] = other[...].astype(F32) / math.sqrt(nodes)


def bits(n):
    return [1 << b for b in range(n.bit_length() - 1)]


def tree(terms):
    while len(terms) > 1:
        terms = [terms[i] + terms[i + 1] for i in range(0, len(terms), 2)]
    return terms[0]


def body(features, weight, cotangent, block_index, block_count, block_values):
    nrow, ncol = lax.axis_size("row"), lax.axis_size("col")
    rows, width = features.shape
    size = block_values.shape[-1]
    slots = block_values.shape[2]
    zs = ncol // 2
    part = width // 2
    shape = jax.ShapeDtypeStruct

    def over_row(x, s):
        return move(x, nrow, ncol, lambda r, c: (r ^ s, c))

    def over_col(x, s):
        return move(x, nrow, ncol, lambda r, c: (r, c ^ s))

    idx = block_index.reshape(slots)
    cnt = block_count.reshape(1)
    vals = block_values.reshape(slots, size, size)
    vals1 = over_col(vals, 1)
    vals = pltpu.with_memory_space_constraint(vals, pltpu.HBM)
    idx1 = over_col(idx, 1)
    cnt1 = over_col(cnt, 1)
    cots = [cotangent, over_col(cotangent, 1)]
    feats = [features] + [over_row(features, s) for s in range(1, nrow)]
    for s in range(1, zs):
        got = over_col(cotangent, 2 * s)
        cots += [got, over_col(got, 1)]
    feats1 = [over_col(feats[s], 1) for s in range(nrow)]
    feats[0] = pltpu.with_memory_space_constraint(features, pltpu.HBM)
    cots[0] = pltpu.with_memory_space_constraint(cotangent, pltpu.HBM)

    parts = pl.pallas_call(
        functools.partial(fwd_kernel, nrow, ncol),
        out_shape=[shape((rows, width), BF16)] * zs,
        in_specs=[SMEM] * 4 + [HBM, ANY, HBM] + [ANY] * (2 * nrow - 1),
        out_specs=[VMEM] * zs,
        scratch_shapes=[
            pltpu.VMEM((2 * slots, size, size), BF16),
            pltpu.VMEM((2 * nrow * rows, width), BF16),
            pltpu.VMEM((zs * rows + size, width), F32),
            pltpu.SMEM((3, 2 * slots + UNROLL), jnp.int32),
            pltpu.SemaphoreType.DMA((2 * nrow + 2,)),
        ],
        compiler_params=pltpu.CompilerParams(vmem_limit_bytes=16 << 20),
        name="fwd_tile",
    )(idx, idx1, cnt, cnt1, vals, vals1, *feats, *feats1)
    parts = [parts[0]] + [over_col(parts[s], 2 * s) for s in range(1, zs)]
    hidden = pl.pallas_call(
        functools.partial(sum_dot_kernel, zs, (((1,), (0,)), ((), ()))),
        out_shape=shape((rows, width), BF16),
        in_specs=[VMEM] * (1 + zs),
        out_specs=VMEM,
        compiler_params=pltpu.CompilerParams(vmem_limit_bytes=8 << 20),
        name="hidden",
    )(weight, *parts)

    out = pl.pallas_call(
        functools.partial(bwd_kernel, nrow, ncol),
        out_shape=[shape((rows, width), BF16)] * nrow + [shape((part, width), BF16)] * 2,
        in_specs=[SMEM, SMEM, HBM, HBM] + [ANY] * (nrow - 1) + [HBM] + [ANY] * (ncol - 1),
        out_specs=[VMEM] * (nrow + 2),
        scratch_shapes=[
            pltpu.VMEM((slots, size, size), BF16),
            pltpu.VMEM((nrow * rows, width), BF16),
            pltpu.VMEM((ncol * rows, width), BF16),
            pltpu.VMEM((nrow * rows + size, width), F32),
            pltpu.VMEM((width, width), F32),
            pltpu.SemaphoreType.DMA((nrow + ncol + 1,)),
        ],
        compiler_params=pltpu.CompilerParams(vmem_limit_bytes=16 << 20),
        name="bwd_tile",
    )(idx, cnt, vals, *feats, *cots)
    backs, term, send = out[:nrow], out[nrow], out[nrow + 1]
    backs = [backs[0]] + [over_row(backs[s], s) for s in range(1, nrow)]
    input_grad = pl.pallas_call(
        functools.partial(sum_dot_kernel, nrow, (((1,), (1,)), ((), ()))),
        out_shape=shape((rows, width), BF16),
        in_specs=[VMEM] * (1 + nrow),
        out_specs=VMEM,
        compiler_params=pltpu.CompilerParams(vmem_limit_bytes=8 << 20),
        name="input_grad",
    )(weight, *backs)

    term = term + over_col(send, 1)
    term = tree([term] + [over_row(term, s) for s in range(1, nrow)])
    for s in bits(zs):
        term = term + over_col(term, 2 * s)
    weight_grad = pl.pallas_call(
        functools.partial(join_kernel, rows * nrow * ncol),
        out_shape=shape((width, width), F32),
        in_specs=[VMEM, VMEM],
        out_specs=VMEM,
        compiler_params=pltpu.CompilerParams(vmem_limit_bytes=8 << 20),
        name="weight_grad",
    )(term, over_col(term, 1))
    return (hidden, input_grad, weight_grad)


def solution(mesh):
    in_specs = (
        P(("col", "row"), None),
        P(),
        P(("row", "col"), None),
        P("row", "col", None),
        P("row", "col"),
        P("row", "col", None, None, None),
    )
    out_specs = (P(("row", "col"), None), P(("col", "row"), None), P())

    return jax.shard_map(body, mesh=mesh, in_specs=in_specs, out_specs=out_specs, check_vma=False)
```

```python
import functools
import math

import jax
import jax.numpy as jnp
from jax import lax
from jax.experimental import pallas as pl
from jax.experimental.pallas import tpu as pltpu
from jax.sharding import PartitionSpec as P


AXES = ("row", "col")
F32 = jnp.float32
BF16 = jnp.bfloat16
UNROLL = 4
ANY = pl.BlockSpec(memory_space=pl.ANY)
HBM = pl.BlockSpec(memory_space=pltpu.HBM)
VMEM = pl.BlockSpec(memory_space=pltpu.VMEM)


def move(x, rows, cols, fn):
    pairs = []
    for r in range(rows):
        for c in range(cols):
            to = fn(r, c)
            if to is not None:
                pairs.append((r * cols + c, to[0] * cols + to[1]))
    return lax.ppermute(x, AXES, pairs)


def fwd_kernel(nrow, ncol, idx0_hbm, idx1_hbm, cnt0_hbm, cnt1_hbm, vals0, vals1, *rest):
    shards = rest[:2 * nrow]
    zs = ncol // 2
    outs = rest[2 * nrow:2 * nrow + zs]
    vbuf, fbuf, acc, todo, idx0, idx1, cnt0, cnt1, sem, meta_sem = rest[2 * nrow + zs:]
    slots, size = vals0.shape[0], vals0.shape[1]
    rows, _ = shards[0].shape
    per = rows // size
    block_cols = nrow * per
    full = zs * rows
    me_r = lax.axis_index("row")
    me_c = lax.axis_index("col")
    me_z, me_k = me_c // 2, me_c % 2
    pairs = ((idx0_hbm, idx0), (idx1_hbm, idx1), (cnt0_hbm, cnt0), (cnt1_hbm, cnt1))
    metas = [pltpu.make_async_copy(src, dst, meta_sem.at[i]) for i, (src, dst) in enumerate(pairs)]
    for copy in metas:
        copy.start()
    copies = []
    for t, vals in enumerate((vals0, vals1)):
        copies.append(pltpu.make_async_copy(vals, vbuf.at[pl.ds(t * slots, slots)], sem.at[2 * nrow + t]))
        for s in range(nrow):
            at = pl.multiple_of((me_r ^ s) * rows + t * nrow * rows, rows)
            n = t * nrow + s
            copies.append(pltpu.make_async_copy(shards[n], fbuf.at[pl.ds(at, rows)], sem.at[n]))
    for copy in copies:
        copy.start()
    acc[...] = jnp.zeros_like(acc)

    for copy in metas:
        copy.wait()

    def listed(t, idx, cnt, n):
        def one(g, n):
            q = idx[g]
            br, bc = q // block_cols, q % block_cols
            owner = br // per
            todo[0, n] = t * slots + g
            todo[1, n] = t * nrow * rows + bc * size
            todo[2, n] = ((owner // 2) ^ me_z) * rows + (br % per) * size
            return n + jnp.where(owner % 2 == me_k, 1, 0)

        return lax.fori_loop(0, cnt[0], one, n)

    count = listed(1, idx1, cnt1, listed(0, idx0, cnt0, 0))
    for u in range(UNROLL):
        todo[0, count + u] = 0
        todo[1, count + u] = 0
        todo[2, count + u] = full
    for copy in copies:
        copy.wait()

    def group(i, carry):
        prods = []
        for u in range(UNROLL):
            g = i * UNROLL + u
            block = fbuf[pl.ds(pl.multiple_of(todo[1, g], size), size), :]
            prods.append((pl.multiple_of(todo[2, g], size), jnp.dot(vbuf[todo[0, g]], block, preferred_element_type=F32)))
        for at, out in prods:
            acc[pl.ds(at, size), :] += out
        return carry

    lax.fori_loop(0, (count + UNROLL - 1) // UNROLL, group, 0)
    for s in range(zs):
        outs[s][...] = acc[s * rows:(s + 1) * rows, :].astype(BF16)


def bwd_kernel(nrow, ncol, idx_hbm, cnt_hbm, vals, *rest):
    feats = rest[:nrow]
    cots = rest[nrow:nrow + ncol]
    outs = rest[nrow + ncol:2 * nrow + ncol]
    tkeep, tsend, vbuf, fbuf, cbuf, acc, tbuf, idx, cnt, sem, meta_sem = rest[2 * nrow + ncol:]
    size = vals.shape[1]
    rows, width = feats[0].shape
    per = rows // size
    block_cols = nrow * per
    full = nrow * rows
    me_r = lax.axis_index("row")
    me_c = lax.axis_index("col")
    me_k = me_c % 2
    metas = [pltpu.make_async_copy(idx_hbm, idx, meta_sem.at[0]), pltpu.make_async_copy(cnt_hbm, cnt, meta_sem.at[1])]
    copies = metas + [pltpu.make_async_copy(vals, vbuf, sem.at[nrow + ncol])]
    for s in range(nrow):
        copies.append(pltpu.make_async_copy(feats[s], fbuf.at[pl.ds(s * rows, rows)], sem.at[s]))
    for s in range(ncol):
        at = pl.multiple_of((me_c ^ s) * rows, rows)
        copies.append(pltpu.make_async_copy(cots[s], cbuf.at[pl.ds(at, rows)], sem.at[nrow + s]))
    for copy in copies:
        copy.start()
    acc[...] = jnp.zeros_like(acc)
    for copy in copies:
        copy.wait()
    count = cnt[0]

    def group(i, carry):
        prods = []
        for u in range(UNROLL):
            g = i * UNROLL + u
            q = idx[g]
            br, bc = q // block_cols, q % block_cols
            at = ((bc // per) ^ me_r) * rows + (bc % per) * size
            at = pl.multiple_of(jnp.where(g < count, at, full), size)
            block = cbuf[pl.ds(pl.multiple_of(br * size, size), size), :]
            prods.append((at, lax.dot_general(vbuf[g], block, (((0,), (0,)), ((), ())), preferred_element_type=F32)))
        for at, out in prods:
            acc[pl.ds(at, size), :] += out
        return carry

    lax.fori_loop(0, (count + UNROLL - 1) // UNROLL, group, 0)
    term = jnp.zeros((width, width), F32)
    for s in range(nrow):
        back = acc[s * rows:(s + 1) * rows, :].astype(BF16)
        outs[s][...] = back
        term += lax.dot_general(
            fbuf[s * rows:(s + 1) * rows, :], back, (((0,), (0,)), ((), ())), preferred_element_type=F32
        )
    tbuf[...] = term
    part = width // 2
    tkeep[...] = tbuf[pl.ds(pl.multiple_of(me_k * part, part), part), :].astype(BF16)
    tsend[...] = tbuf[pl.ds(pl.multiple_of((1 - me_k) * part, part), part), :].astype(BF16)


def split_dot(x, w, dims):
    hi = x.astype(BF16)
    lo = (x - hi.astype(F32)).astype(BF16)
    return lax.dot_general(hi, w, dims, preferred_element_type=F32) + lax.dot_general(
        lo, w, dims, preferred_element_type=F32
    )


def sum_dot_kernel(parts, dims, w, *rest):
    total = rest[0][...].astype(F32)
    for s in range(1, parts):
        total += rest[s][...].astype(F32)
    rest[parts][...] = split_dot(total, w[...], dims).astype(BF16)


def join_kernel(nodes, mine, other, out):
    part = mine.shape[0]
    me_k = lax.axis_index("col") % 2
    out[pl.ds(pl.multiple_of(me_k * part, part), part), :] = mine[...].astype(F32) / math.sqrt(nodes)
    out[pl.ds(pl.multiple_of((1 - me_k) * part, part), part), :] = other[...].astype(F32) / math.sqrt(nodes)


def bits(n):
    return [1 << b for b in range(n.bit_length() - 1)]


def ones(s):
    return s.bit_count()


def tree(terms):
    while len(terms) > 1:
        terms = [terms[i] + terms[i + 1] for i in range(0, len(terms), 2)]
    return terms[0]


def body(features, weight, cotangent, block_index, block_count, block_values):
    nrow, ncol = lax.axis_size("row"), lax.axis_size("col")
    rows, width = features.shape
    size = block_values.shape[-1]
    slots = block_values.shape[2]
    zs = ncol // 2
    part = width // 2
    shape = jax.ShapeDtypeStruct

    def over_row(x, s):
        return move(x, nrow, ncol, lambda r, c: (r ^ s, c))

    def over_col(x, s):
        return move(x, nrow, ncol, lambda r, c: (r, c ^ s))

    idx = block_index.reshape(slots)
    cnt = block_count.reshape(1)
    vals = block_values.reshape(slots, size, size)
    vals1 = over_col(vals, 1)
    vals = pltpu.with_memory_space_constraint(vals, pltpu.HBM)
    idx1 = over_col(idx, 1)
    cnt1 = over_col(cnt, 1)
    cots = [cotangent, over_col(cotangent, 1)]
    feats = [features] + [over_row(features, s) for s in range(1, nrow)]
    cots += [None] * (ncol - 2)
    for s in sorted(range(1, zs), key=ones):
        low = s & -s
        got = over_col(cots[2 * (s ^ low)], 2 * low)
        cots[2 * s:2 * s + 2] = [got, over_col(got, 1)]
    feats1 = [over_col(feats[s], 1) for s in range(nrow)]
    feats[0] = pltpu.with_memory_space_constraint(features, pltpu.HBM)
    cots[0] = pltpu.with_memory_space_constraint(cotangent, pltpu.HBM)

    parts = pl.pallas_call(
        functools.partial(fwd_kernel, nrow, ncol),
        out_shape=[shape((rows, width), BF16)] * zs,
        in_specs=[ANY] * 4 + [HBM, ANY, HBM] + [ANY] * (2 * nrow - 1),
        out_specs=[VMEM] * zs,
        scratch_shapes=[
            pltpu.VMEM((2 * slots, size, size), BF16),
            pltpu.VMEM((2 * nrow * rows, width), BF16),
            pltpu.VMEM((zs * rows + size, width), F32),
            pltpu.SMEM((3, 2 * slots + UNROLL), jnp.int32),
            pltpu.SMEM((slots,), jnp.int32),
            pltpu.SMEM((slots,), jnp.int32),
            pltpu.SMEM((1,), jnp.int32),
            pltpu.SMEM((1,), jnp.int32),
            pltpu.SemaphoreType.DMA((2 * nrow + 2,)),
            pltpu.SemaphoreType.DMA((4,)),
        ],
        compiler_params=pltpu.CompilerParams(vmem_limit_bytes=16 << 20),
        name="fwd_tile",
    )(idx, idx1, cnt, cnt1, vals, vals1, *feats, *feats1)
    parts = list(parts)
    final = [parts[0]]
    for s in sorted(range(1, zs), key=ones, reverse=True):
        low = s & -s
        got = over_col(parts[s], 2 * low)
        if s == low:
            final.append(got)
        else:
            parts[s ^ low] = parts[s ^ low] + got
    parts = final
    hidden = pl.pallas_call(
        functools.partial(sum_dot_kernel, len(parts), (((1,), (0,)), ((), ()))),
        out_shape=shape((rows, width), BF16),
        in_specs=[VMEM] * (1 + len(parts)),
        out_specs=VMEM,
        compiler_params=pltpu.CompilerParams(vmem_limit_bytes=8 << 20),
        name="hidden",
    )(weight, *parts)

    out = pl.pallas_call(
        functools.partial(bwd_kernel, nrow, ncol),
        out_shape=[shape((rows, width), BF16)] * nrow + [shape((part, width), BF16)] * 2,
        in_specs=[ANY, ANY, HBM, HBM] + [ANY] * (nrow - 1) + [HBM] + [ANY] * (ncol - 1),
        out_specs=[VMEM] * (nrow + 2),
        scratch_shapes=[
            pltpu.VMEM((slots, size, size), BF16),
            pltpu.VMEM((nrow * rows, width), BF16),
            pltpu.VMEM((ncol * rows, width), BF16),
            pltpu.VMEM((nrow * rows + size, width), F32),
            pltpu.VMEM((width, width), F32),
            pltpu.SMEM((slots,), jnp.int32),
            pltpu.SMEM((1,), jnp.int32),
            pltpu.SemaphoreType.DMA((nrow + ncol + 1,)),
            pltpu.SemaphoreType.DMA((2,)),
        ],
        compiler_params=pltpu.CompilerParams(vmem_limit_bytes=16 << 20),
        name="bwd_tile",
    )(idx, cnt, vals, *feats, *cots)
    backs, term, send = out[:nrow], out[nrow], out[nrow + 1]
    backs = [backs[0]] + [over_row(backs[s], s) for s in range(1, nrow)]
    input_grad = pl.pallas_call(
        functools.partial(sum_dot_kernel, nrow, (((1,), (1,)), ((), ()))),
        out_shape=shape((rows, width), BF16),
        in_specs=[VMEM] * (1 + nrow),
        out_specs=VMEM,
        compiler_params=pltpu.CompilerParams(vmem_limit_bytes=8 << 20),
        name="input_grad",
    )(weight, *backs)

    term = term + over_col(send, 1)
    term = tree([term] + [over_row(term, s) for s in range(1, nrow)])
    for s in bits(zs):
        term = term + over_col(term, 2 * s)
    weight_grad = pl.pallas_call(
        functools.partial(join_kernel, rows * nrow * ncol),
        out_shape=shape((width, width), F32),
        in_specs=[VMEM, VMEM],
        out_specs=VMEM,
        compiler_params=pltpu.CompilerParams(vmem_limit_bytes=8 << 20),
        name="weight_grad",
    )(term, over_col(term, 1))
    return (hidden, input_grad, weight_grad)


def solution(mesh):
    in_specs = (
        P(("col", "row"), None),
        P(),
        P(("row", "col"), None),
        P("row", "col", None),
        P("row", "col"),
        P("row", "col", None, None, None),
    )
    out_specs = (P(("row", "col"), None), P(("col", "row"), None), P())

    return jax.shard_map(body, mesh=mesh, in_specs=in_specs, out_specs=out_specs, check_vma=False)
```

```python
import functools
import math

import jax
import jax.numpy as jnp
from jax import lax
from jax.experimental import pallas as pl
from jax.experimental.pallas import tpu as pltpu
from jax.sharding import PartitionSpec as P


AXES = ("row", "col")
F32 = jnp.float32
BF16 = jnp.bfloat16
UNROLL = 4
ANY = pl.BlockSpec(memory_space=pl.ANY)
HBM = pl.BlockSpec(memory_space=pltpu.HBM)
VMEM = pl.BlockSpec(memory_space=pltpu.VMEM)
SMEM = pl.BlockSpec(memory_space=pltpu.SMEM)


def move(x, rows, cols, fn):
    pairs = []
    for r in range(rows):
        for c in range(cols):
            to = fn(r, c)
            if to is not None:
                pairs.append((r * cols + c, to[0] * cols + to[1]))
    return lax.ppermute(x, AXES, pairs)


def fwd_blocks(todo, count, vbuf, fbuf, acc, size):
    span = todo.shape[0] // 3

    def group(i, carry):
        prods = []
        for u in range(UNROLL):
            g = i * UNROLL + u
            block = fbuf[pl.ds(pl.multiple_of(todo[span + g], size), size), :]
            at = pl.multiple_of(todo[2 * span + g], size)
            prods.append((at, jnp.dot(vbuf[todo[g]], block, preferred_element_type=F32)))
        for at, out in prods:
            acc[pl.ds(at, size), :] += out
        return carry

    lax.fori_loop(0, (count + UNROLL - 1) // UNROLL, group, 0)


def fwd_first(nrow, ncol, idx0_hbm, idx1_hbm, cnt0_hbm, cnt1_hbm, vals0, vals1, shard0, shard1, *rest):
    acc, later, vbuf, fbuf, todo, idx0, idx1, cnt0, cnt1, sem, meta_sem = rest
    zs = ncol // 2
    slots, size = vals0.shape[0], vals0.shape[1]
    rows, _ = shard0.shape
    per = rows // size
    block_cols = nrow * per
    full = zs * rows
    span = todo.shape[0] // 3
    me_r = lax.axis_index("row")
    me_c = lax.axis_index("col")
    me_z, me_k = me_c // 2, me_c % 2
    pairs = ((idx0_hbm, idx0), (idx1_hbm, idx1), (cnt0_hbm, cnt0), (cnt1_hbm, cnt1))
    metas = [pltpu.make_async_copy(src, dst, meta_sem.at[i]) for i, (src, dst) in enumerate(pairs)]
    copies = []
    for t, (vals, shard) in enumerate(((vals0, shard0), (vals1, shard1))):
        copies.append(pltpu.make_async_copy(vals, vbuf.at[pl.ds(t * slots, slots)], sem.at[2 * t]))
        copies.append(pltpu.make_async_copy(shard, fbuf.at[pl.ds(t * rows, rows)], sem.at[2 * t + 1]))
    for copy in metas + copies:
        copy.start()
    acc[...] = jnp.zeros_like(acc)
    for copy in metas:
        copy.wait()

    def listed(t, idx, cnt, counts):
        def one(g, counts):
            now, late = counts
            q = idx[g]
            br, bc = q // block_cols, q % block_cols
            owner = br // per
            s = (bc // per) ^ me_r
            at = ((owner // 2) ^ me_z) * rows + (br % per) * size
            inside = (bc % per) * size
            mine = owner % 2 == me_k
            todo[now] = t * slots + g
            todo[span + now] = t * rows + inside
            todo[2 * span + now] = at
            later[late] = t * slots + g
            later[span + late] = (t * (nrow - 1) + s - 1) * rows + inside
            later[2 * span + late] = at
            return (
                now + jnp.where(mine & (s == 0), 1, 0),
                late + jnp.where(mine & (s != 0), 1, 0),
            )

        return lax.fori_loop(0, cnt[0], one, counts)

    now, late = listed(1, idx1, cnt1, listed(0, idx0, cnt0, (0, 0)))
    for u in range(UNROLL):
        for ref, n in ((todo, now), (later, late)):
            ref[n + u] = 0
            ref[span + n + u] = 0
            ref[2 * span + n + u] = full
    later[span - 1] = late
    for copy in copies:
        copy.wait()
    fwd_blocks(todo, now, vbuf, fbuf, acc, size)


def fwd_rest(nrow, ncol, acc_in, later_hbm, vals0, vals1, *rest):
    zs = ncol // 2
    shards = rest[:2 * nrow - 2]
    acc = rest[2 * nrow - 2]
    outs = rest[2 * nrow - 1:2 * nrow - 1 + zs]
    vbuf, fbuf, todo, sem = rest[2 * nrow - 1 + zs:]
    slots, size = vals0.shape[0], vals0.shape[1]
    rows, _ = shards[0].shape
    span = todo.shape[0] // 3
    copies = [pltpu.make_async_copy(later_hbm, todo, sem.at[2 * nrow])]
    for t, vals in enumerate((vals0, vals1)):
        copies.append(pltpu.make_async_copy(vals, vbuf.at[pl.ds(t * slots, slots)], sem.at[2 * nrow - 2 + t]))
    for n in range(2 * nrow - 2):
        copies.append(pltpu.make_async_copy(shards[n], fbuf.at[pl.ds(n * rows, rows)], sem.at[n]))
    for copy in copies:
        copy.start()
    for copy in copies:
        copy.wait()
    fwd_blocks(todo, todo[span - 1], vbuf, fbuf, acc, size)
    for s in range(zs):
        outs[s][...] = acc[s * rows:(s + 1) * rows, :].astype(BF16)


def bwd_kernel(nrow, ncol, idx_hbm, cnt_hbm, vals, *rest):
    cots = rest[:ncol]
    outs = rest[ncol:nrow + ncol]
    vbuf, cbuf, acc, idx, cnt, sem = rest[nrow + ncol:]
    size = vals.shape[1]
    rows, _ = cots[0].shape
    per = rows // size
    block_cols = nrow * per
    full = nrow * rows
    me_r = lax.axis_index("row")
    me_c = lax.axis_index("col")
    pairs = ((idx_hbm, idx), (cnt_hbm, cnt), (vals, vbuf))
    copies = [pltpu.make_async_copy(src, dst, sem.at[ncol + i]) for i, (src, dst) in enumerate(pairs)]
    for s in range(ncol):
        at = pl.multiple_of((me_c ^ s) * rows, rows)
        copies.append(pltpu.make_async_copy(cots[s], cbuf.at[pl.ds(at, rows)], sem.at[s]))
    for copy in copies:
        copy.start()
    acc[...] = jnp.zeros_like(acc)
    for copy in copies:
        copy.wait()
    count = cnt[0]

    def group(i, carry):
        prods = []
        for u in range(UNROLL):
            g = i * UNROLL + u
            q = idx[g]
            br, bc = q // block_cols, q % block_cols
            at = ((bc // per) ^ me_r) * rows + (bc % per) * size
            at = pl.multiple_of(jnp.where(g < count, at, full), size)
            block = cbuf[pl.ds(pl.multiple_of(br * size, size), size), :]
            prods.append((at, lax.dot_general(vbuf[g], block, (((0,), (0,)), ((), ())), preferred_element_type=F32)))
        for at, out in prods:
            acc[pl.ds(at, size), :] += out
        return carry

    lax.fori_loop(0, (count + UNROLL - 1) // UNROLL, group, 0)
    for s in range(nrow):
        outs[s][...] = acc[s * rows:(s + 1) * rows, :].astype(BF16)


def term_kernel(zs, *rest):
    tkeep, tsend, tbuf = rest[2 * zs:]
    part = tkeep.shape[0]
    me_k = lax.axis_index("col") % 2
    for s in range(zs):
        out = lax.dot_general(
            rest[s][...], rest[zs + s][...], (((0,), (0,)), ((), ())), preferred_element_type=F32
        )
        tbuf[...] = out if s == 0 else tbuf[...] + out
    tkeep[...] = tbuf[pl.ds(pl.multiple_of(me_k * part, part), part), :].astype(BF16)
    tsend[...] = tbuf[pl.ds(pl.multiple_of((1 - me_k) * part, part), part), :].astype(BF16)


def split_dot(x, w, dims):
    hi = x.astype(BF16)
    lo = (x - hi.astype(F32)).astype(BF16)
    return lax.dot_general(hi, w, dims, preferred_element_type=F32) + lax.dot_general(
        lo, w, dims, preferred_element_type=F32
    )


def sum_dot_kernel(parts, dims, w, *rest):
    total = rest[0][...].astype(F32)
    for s in range(1, parts):
        total += rest[s][...].astype(F32)
    rest[parts][...] = split_dot(total, w[...], dims).astype(BF16)


def join_kernel(nodes, mine, other, out):
    part = mine.shape[0]
    me_k = lax.axis_index("col") % 2
    out[pl.ds(pl.multiple_of(me_k * part, part), part), :] = mine[...].astype(F32) / math.sqrt(nodes)
    out[pl.ds(pl.multiple_of((1 - me_k) * part, part), part), :] = other[...].astype(F32) / math.sqrt(nodes)


def bits(n):
    return [1 << b for b in range(n.bit_length() - 1)]


def ones(s):
    return s.bit_count()


def body(features, weight, cotangent, block_index, block_count, block_values):
    nrow, ncol = lax.axis_size("row"), lax.axis_size("col")
    rows, width = features.shape
    size = block_values.shape[-1]
    slots = block_values.shape[2]
    zs = ncol // 2
    part = width // 2
    shape = jax.ShapeDtypeStruct

    def over_row(x, s):
        return move(x, nrow, ncol, lambda r, c: (r ^ s, c))

    def over_col(x, s):
        return move(x, nrow, ncol, lambda r, c: (r, c ^ s))

    idx = block_index.reshape(slots)
    cnt = block_count.reshape(1)
    vals = block_values.reshape(slots, size, size)
    vals1 = over_col(vals, 1)
    vals = pltpu.with_memory_space_constraint(vals, pltpu.HBM)
    idx1 = over_col(idx, 1)
    cnt1 = over_col(cnt, 1)
    cots = [cotangent, over_col(cotangent, 1)]
    feats = [features] + [over_row(features, s) for s in range(1, nrow)]
    cots += [None] * (ncol - 2)
    for s in sorted(range(1, zs), key=ones):
        low = s & -s
        got = over_col(cots[2 * (s ^ low)], 2 * low)
        cots[2 * s:2 * s + 2] = [got, over_col(got, 1)]
    feats1 = [over_col(feats[s], 1) for s in range(nrow)]
    feats[0] = pltpu.with_memory_space_constraint(features, pltpu.HBM)
    cots[0] = pltpu.with_memory_space_constraint(cotangent, pltpu.HBM)

    span = 2 * slots + 2 * UNROLL
    acc, later = pl.pallas_call(
        functools.partial(fwd_first, nrow, ncol),
        out_shape=[shape((zs * rows + size, width), F32), shape((3 * span,), jnp.int32)],
        in_specs=[ANY] * 4 + [HBM, ANY, HBM, ANY],
        out_specs=[VMEM, SMEM],
        scratch_shapes=[
            pltpu.VMEM((2 * slots, size, size), BF16),
            pltpu.VMEM((2 * rows, width), BF16),
            pltpu.SMEM((3 * span,), jnp.int32),
            pltpu.SMEM((slots,), jnp.int32),
            pltpu.SMEM((slots,), jnp.int32),
            pltpu.SMEM((1,), jnp.int32),
            pltpu.SMEM((1,), jnp.int32),
            pltpu.SemaphoreType.DMA((4,)),
            pltpu.SemaphoreType.DMA((4,)),
        ],
        compiler_params=pltpu.CompilerParams(vmem_limit_bytes=12 << 20),
        name="fwd_first",
    )(idx, idx1, cnt, cnt1, vals, vals1, feats[0], feats1[0])
    parts = pl.pallas_call(
        functools.partial(fwd_rest, nrow, ncol),
        out_shape=[shape(acc.shape, F32)] + [shape((rows, width), BF16)] * zs,
        in_specs=[VMEM, ANY, HBM, ANY] + [ANY] * (2 * nrow - 2),
        out_specs=[VMEM] * (1 + zs),
        scratch_shapes=[
            pltpu.VMEM((2 * slots, size, size), BF16),
            pltpu.VMEM(((2 * nrow - 2) * rows, width), BF16),
            pltpu.SMEM((3 * span,), jnp.int32),
            pltpu.SemaphoreType.DMA((2 * nrow + 1,)),
        ],
        input_output_aliases={0: 0},
        compiler_params=pltpu.CompilerParams(vmem_limit_bytes=16 << 20),
        name="fwd_tile",
    )(acc, later, vals, vals1, *feats[1:], *feats1[1:])[1:]
    term, send = pl.pallas_call(
        functools.partial(term_kernel, zs),
        out_shape=[shape((part, width), BF16)] * 2,
        in_specs=[VMEM] * (2 * zs),
        out_specs=[VMEM] * 2,
        scratch_shapes=[pltpu.VMEM((width, width), F32)],
        compiler_params=pltpu.CompilerParams(vmem_limit_bytes=8 << 20),
        name="weight_term",
    )(*parts, cotangent, *cots[2::2])
    parts = list(parts)
    final = [parts[0]]
    for s in sorted(range(1, zs), key=ones, reverse=True):
        low = s & -s
        got = over_col(parts[s], 2 * low)
        if s == low:
            final.append(got)
        else:
            parts[s ^ low] = parts[s ^ low] + got
    parts = final
    hidden = pl.pallas_call(
        functools.partial(sum_dot_kernel, len(parts), (((1,), (0,)), ((), ()))),
        out_shape=shape((rows, width), BF16),
        in_specs=[VMEM] * (1 + len(parts)),
        out_specs=VMEM,
        compiler_params=pltpu.CompilerParams(vmem_limit_bytes=8 << 20),
        name="hidden",
    )(weight, *parts)

    backs = pl.pallas_call(
        functools.partial(bwd_kernel, nrow, ncol),
        out_shape=[shape((rows, width), BF16)] * nrow,
        in_specs=[ANY, ANY, HBM, HBM] + [ANY] * (ncol - 1),
        out_specs=[VMEM] * nrow,
        scratch_shapes=[
            pltpu.VMEM((slots, size, size), BF16),
            pltpu.VMEM((ncol * rows, width), BF16),
            pltpu.VMEM((nrow * rows + size, width), F32),
            pltpu.SMEM((slots,), jnp.int32),
            pltpu.SMEM((1,), jnp.int32),
            pltpu.SemaphoreType.DMA((ncol + 3,)),
        ],
        compiler_params=pltpu.CompilerParams(vmem_limit_bytes=16 << 20),
        name="bwd_tile",
    )(idx, cnt, vals, *cots)
    backs = [backs[0]] + [over_row(backs[s], s) for s in range(1, nrow)]
    input_grad = pl.pallas_call(
        functools.partial(sum_dot_kernel, nrow, (((1,), (1,)), ((), ()))),
        out_shape=shape((rows, width), BF16),
        in_specs=[VMEM] * (1 + nrow),
        out_specs=VMEM,
        compiler_params=pltpu.CompilerParams(vmem_limit_bytes=8 << 20),
        name="input_grad",
    )(weight, *backs)

    term = term + over_col(send, 1)
    for s in bits(nrow):
        term = term + over_row(term, s)
    for s in bits(zs):
        term = term + over_col(term, 2 * s)
    weight_grad = pl.pallas_call(
        functools.partial(join_kernel, rows * nrow * ncol),
        out_shape=shape((width, width), F32),
        in_specs=[VMEM, VMEM],
        out_specs=VMEM,
        compiler_params=pltpu.CompilerParams(vmem_limit_bytes=8 << 20),
        name="weight_grad",
    )(term, over_col(term, 1))
    return (hidden, input_grad, weight_grad)


def solution(mesh):
    in_specs = (
        P(("col", "row"), None),
        P(),
        P(("row", "col"), None),
        P("row", "col", None),
        P("row", "col"),
        P("row", "col", None, None, None),
    )
    out_specs = (P(("row", "col"), None), P(("col", "row"), None), P())

    return jax.shard_map(body, mesh=mesh, in_specs=in_specs, out_specs=out_specs, check_vma=False)
```

```python
import functools
import math

import jax
import jax.numpy as jnp
from jax import lax
from jax.experimental import pallas as pl
from jax.experimental.pallas import tpu as pltpu
from jax.sharding import PartitionSpec as P


AXES = ("row", "col")
F32 = jnp.float32
BF16 = jnp.bfloat16
UNROLL = 16
ANY = pl.BlockSpec(memory_space=pl.ANY)
HBM = pl.BlockSpec(memory_space=pltpu.HBM)
VMEM = pl.BlockSpec(memory_space=pltpu.VMEM)


def move(x, rows, cols, fn):
    pairs = []
    for r in range(rows):
        for c in range(cols):
            to = fn(r, c)
            if to is not None:
                pairs.append((r * cols + c, to[0] * cols + to[1]))
    return lax.ppermute(x, AXES, pairs)


def fwd_kernel(nrow, ncol, idx0_hbm, idx1_hbm, cnt0_hbm, cnt1_hbm, vals0, vals1, *rest):
    shards = rest[:2 * nrow]
    zs = ncol // 2
    outs = rest[2 * nrow:2 * nrow + zs]
    vbuf, fbuf, acc, todo, idx0, idx1, cnt0, cnt1, sem, meta_sem = rest[2 * nrow + zs:]
    slots, size = vals0.shape[0], vals0.shape[1]
    rows, _ = shards[0].shape
    per = rows // size
    block_cols = nrow * per
    full = zs * rows
    me_r = lax.axis_index("row")
    me_c = lax.axis_index("col")
    me_z, me_k = me_c // 2, me_c % 2
    pairs = ((idx0_hbm, idx0), (idx1_hbm, idx1), (cnt0_hbm, cnt0), (cnt1_hbm, cnt1))
    metas = [pltpu.make_async_copy(src, dst, meta_sem.at[i]) for i, (src, dst) in enumerate(pairs)]
    for copy in metas:
        copy.start()
    copies = []
    for t, vals in enumerate((vals0, vals1)):
        copies.append(pltpu.make_async_copy(vals, vbuf.at[pl.ds(t * slots, slots)], sem.at[2 * nrow + t]))
        for s in range(nrow):
            at = pl.multiple_of((me_r ^ s) * rows + t * nrow * rows, rows)
            n = t * nrow + s
            copies.append(pltpu.make_async_copy(shards[n], fbuf.at[pl.ds(at, rows)], sem.at[n]))
    for copy in copies:
        copy.start()
    acc[...] = jnp.zeros_like(acc)

    for copy in metas:
        copy.wait()

    def listed(t, idx, cnt, n):
        def one(g, n):
            q = idx[g]
            br, bc = q // block_cols, q % block_cols
            owner = br // per
            todo[0, n] = t * slots + g
            todo[1, n] = t * nrow * rows + bc * size
            todo[2, n] = ((owner // 2) ^ me_z) * rows + (br % per) * size
            return n + jnp.where(owner % 2 == me_k, 1, 0)

        return lax.fori_loop(0, cnt[0], one, n)

    count = listed(1, idx1, cnt1, listed(0, idx0, cnt0, 0))
    for u in range(UNROLL):
        todo[0, count + u] = 0
        todo[1, count + u] = 0
        todo[2, count + u] = full
    for copy in copies:
        copy.wait()

    def group(i, carry):
        prods = []
        for u in range(UNROLL):
            g = i * UNROLL + u
            block = fbuf[pl.ds(pl.multiple_of(todo[1, g], size), size), :]
            prods.append((pl.multiple_of(todo[2, g], size), jnp.dot(vbuf[todo[0, g]], block, preferred_element_type=F32)))
        for at, out in prods:
            acc[pl.ds(at, size), :] += out
        return carry

    lax.fori_loop(0, (count + UNROLL - 1) // UNROLL, group, 0)
    for s in range(zs):
        outs[s][...] = acc[s * rows:(s + 1) * rows, :].astype(BF16)


def bwd_kernel(nrow, ncol, idx_hbm, cnt_hbm, vals, *rest):
    cots = rest[:ncol]
    outs = rest[ncol:nrow + ncol]
    vbuf, cbuf, acc, idx, cnt, sem = rest[nrow + ncol:]
    size = vals.shape[1]
    rows, _ = cots[0].shape
    per = rows // size
    block_cols = nrow * per
    full = nrow * rows
    me_r = lax.axis_index("row")
    me_c = lax.axis_index("col")
    pairs = ((idx_hbm, idx), (cnt_hbm, cnt), (vals, vbuf))
    copies = [pltpu.make_async_copy(src, dst, sem.at[ncol + i]) for i, (src, dst) in enumerate(pairs)]
    for s in range(ncol):
        at = pl.multiple_of((me_c ^ s) * rows, rows)
        copies.append(pltpu.make_async_copy(cots[s], cbuf.at[pl.ds(at, rows)], sem.at[s]))
    for copy in copies:
        copy.start()
    acc[...] = jnp.zeros_like(acc)
    for copy in copies:
        copy.wait()
    count = cnt[0]

    def group(i, carry):
        prods = []
        for u in range(UNROLL):
            g = i * UNROLL + u
            q = idx[g]
            br, bc = q // block_cols, q % block_cols
            at = ((bc // per) ^ me_r) * rows + (bc % per) * size
            at = pl.multiple_of(jnp.where(g < count, at, full), size)
            block = cbuf[pl.ds(pl.multiple_of(br * size, size), size), :]
            prods.append((at, lax.dot_general(vbuf[g], block, (((0,), (0,)), ((), ())), preferred_element_type=F32)))
        for at, out in prods:
            acc[pl.ds(at, size), :] += out
        return carry

    lax.fori_loop(0, (count + UNROLL - 1) // UNROLL, group, 0)
    for s in range(nrow):
        outs[s][...] = acc[s * rows:(s + 1) * rows, :].astype(BF16)


def term_kernel(zs, *rest):
    tkeep, tsend, tbuf = rest[2 * zs:]
    part = tkeep.shape[0]
    me_k = lax.axis_index("col") % 2
    for s in range(zs):
        out = lax.dot_general(
            rest[s][...], rest[zs + s][...], (((0,), (0,)), ((), ())), preferred_element_type=F32
        )
        tbuf[...] = out if s == 0 else tbuf[...] + out
    tkeep[...] = tbuf[pl.ds(pl.multiple_of(me_k * part, part), part), :].astype(BF16)
    tsend[...] = tbuf[pl.ds(pl.multiple_of((1 - me_k) * part, part), part), :].astype(BF16)


def split_dot(x, w, dims):
    hi = x.astype(BF16)
    lo = (x - hi.astype(F32)).astype(BF16)
    return lax.dot_general(hi, w, dims, preferred_element_type=F32) + lax.dot_general(
        lo, w, dims, preferred_element_type=F32
    )


def sum_dot_kernel(parts, dims, w, *rest):
    total = rest[0][...].astype(F32)
    for s in range(1, parts):
        total += rest[s][...].astype(F32)
    rest[parts][...] = split_dot(total, w[...], dims).astype(BF16)


def join_kernel(nodes, mine, other, out):
    part = mine.shape[0]
    me_k = lax.axis_index("col") % 2
    out[pl.ds(pl.multiple_of(me_k * part, part), part), :] = mine[...].astype(F32) / math.sqrt(nodes)
    out[pl.ds(pl.multiple_of((1 - me_k) * part, part), part), :] = other[...].astype(F32) / math.sqrt(nodes)


def bits(n):
    return [1 << b for b in range(n.bit_length() - 1)]


def ones(s):
    return s.bit_count()


def body(features, weight, cotangent, block_index, block_count, block_values):
    nrow, ncol = lax.axis_size("row"), lax.axis_size("col")
    rows, width = features.shape
    size = block_values.shape[-1]
    slots = block_values.shape[2]
    zs = ncol // 2
    part = width // 2
    shape = jax.ShapeDtypeStruct

    def over_row(x, s):
        return move(x, nrow, ncol, lambda r, c: (r ^ s, c))

    def over_col(x, s):
        return move(x, nrow, ncol, lambda r, c: (r, c ^ s))

    idx = block_index.reshape(slots)
    cnt = block_count.reshape(1)
    vals = block_values.reshape(slots, size, size)
    vals1 = over_col(vals, 1)
    vals = pltpu.with_memory_space_constraint(vals, pltpu.HBM)
    idx1 = over_col(idx, 1)
    cnt1 = over_col(cnt, 1)
    cots = [cotangent, over_col(cotangent, 1)]
    feats = [features] + [over_row(features, s) for s in range(1, nrow)]
    cots += [None] * (ncol - 2)
    for s in sorted(range(1, zs), key=ones):
        low = s & -s
        got = over_col(cots[2 * (s ^ low)], 2 * low)
        cots[2 * s:2 * s + 2] = [got, over_col(got, 1)]
    feats1 = [over_col(feats[s], 1) for s in range(nrow)]
    feats[0] = pltpu.with_memory_space_constraint(features, pltpu.HBM)
    cots[0] = pltpu.with_memory_space_constraint(cotangent, pltpu.HBM)

    parts = pl.pallas_call(
        functools.partial(fwd_kernel, nrow, ncol),
        out_shape=[shape((rows, width), BF16)] * zs,
        in_specs=[ANY] * 4 + [HBM, ANY, HBM] + [ANY] * (2 * nrow - 1),
        out_specs=[VMEM] * zs,
        scratch_shapes=[
            pltpu.VMEM((2 * slots, size, size), BF16),
            pltpu.VMEM((2 * nrow * rows, width), BF16),
            pltpu.VMEM((zs * rows + size, width), F32),
            pltpu.SMEM((3, 2 * slots + UNROLL), jnp.int32),
            pltpu.SMEM((slots,), jnp.int32),
            pltpu.SMEM((slots,), jnp.int32),
            pltpu.SMEM((1,), jnp.int32),
            pltpu.SMEM((1,), jnp.int32),
            pltpu.SemaphoreType.DMA((2 * nrow + 2,)),
            pltpu.SemaphoreType.DMA((4,)),
        ],
        compiler_params=pltpu.CompilerParams(vmem_limit_bytes=16 << 20),
        name="fwd_tile",
    )(idx, idx1, cnt, cnt1, vals, vals1, *feats, *feats1)
    term, send = pl.pallas_call(
        functools.partial(term_kernel, zs),
        out_shape=[shape((part, width), BF16)] * 2,
        in_specs=[VMEM] * (2 * zs),
        out_specs=[VMEM] * 2,
        scratch_shapes=[pltpu.VMEM((width, width), F32)],
        compiler_params=pltpu.CompilerParams(vmem_limit_bytes=8 << 20),
        name="weight_term",
    )(*parts, cotangent, *cots[2::2])
    parts = list(parts)
    final = [parts[0]]
    for s in sorted(range(1, zs), key=ones, reverse=True):
        low = s & -s
        got = over_col(parts[s], 2 * low)
        if s == low:
            final.append(got)
        else:
            parts[s ^ low] = parts[s ^ low] + got
    parts = final
    hidden = pl.pallas_call(
        functools.partial(sum_dot_kernel, len(parts), (((1,), (0,)), ((), ()))),
        out_shape=shape((rows, width), BF16),
        in_specs=[VMEM] * (1 + len(parts)),
        out_specs=VMEM,
        compiler_params=pltpu.CompilerParams(vmem_limit_bytes=8 << 20),
        name="hidden",
    )(weight, *parts)

    backs = pl.pallas_call(
        functools.partial(bwd_kernel, nrow, ncol),
        out_shape=[shape((rows, width), BF16)] * nrow,
        in_specs=[ANY, ANY, HBM, HBM] + [ANY] * (ncol - 1),
        out_specs=[VMEM] * nrow,
        scratch_shapes=[
            pltpu.VMEM((slots, size, size), BF16),
            pltpu.VMEM((ncol * rows, width), BF16),
            pltpu.VMEM((nrow * rows + size, width), F32),
            pltpu.SMEM((slots,), jnp.int32),
            pltpu.SMEM((1,), jnp.int32),
            pltpu.SemaphoreType.DMA((ncol + 3,)),
        ],
        compiler_params=pltpu.CompilerParams(vmem_limit_bytes=16 << 20),
        name="bwd_tile",
    )(idx, cnt, vals, *cots)
    backs = [backs[0]] + [over_row(backs[s], s) for s in range(1, nrow)]
    input_grad = pl.pallas_call(
        functools.partial(sum_dot_kernel, nrow, (((1,), (1,)), ((), ()))),
        out_shape=shape((rows, width), BF16),
        in_specs=[VMEM] * (1 + nrow),
        out_specs=VMEM,
        compiler_params=pltpu.CompilerParams(vmem_limit_bytes=8 << 20),
        name="input_grad",
    )(weight, *backs)

    term = term + over_col(send, 1)
    for s in bits(nrow):
        term = term + over_row(term, s)
    for s in bits(zs):
        term = term + over_col(term, 2 * s)
    weight_grad = pl.pallas_call(
        functools.partial(join_kernel, rows * nrow * ncol),
        out_shape=shape((width, width), F32),
        in_specs=[VMEM, VMEM],
        out_specs=VMEM,
        compiler_params=pltpu.CompilerParams(vmem_limit_bytes=8 << 20),
        name="weight_grad",
    )(term, over_col(term, 1))
    return (hidden, input_grad, weight_grad)


def solution(mesh):
    in_specs = (
        P(("col", "row"), None),
        P(),
        P(("row", "col"), None),
        P("row", "col", None),
        P("row", "col"),
        P("row", "col", None, None, None),
    )
    out_specs = (P(("row", "col"), None), P(("col", "row"), None), P())

    return jax.shard_map(body, mesh=mesh, in_specs=in_specs, out_specs=out_specs, check_vma=False)
```
